32 devices in a mesh: ctx: 16 (over z, y, x), dp: 2 (over core).
Axes of the slice: x: 2, y: 2, z: 4, core: 2. Of those that a mesh axis runs over, the one named last changes fastest.
Arguments:
- inputs: bfloat16 [2, 2048, 12288], P('dp', 'ctx'), may hold values from -6 to 6
- feat_weight: float32 [7, 12288], P(None, 'dp'), may hold values from -2 to 2
- filter_taps: float32 [128, 4096], P(None, 'dp'), may hold values from -0.5 to 0.5
- upstream: bfloat16 [2, 2048, 4096], P('dp', 'ctx'), may hold values from -6 to 6
Outputs:
- filter_grad: float32 [128, 4096], P(None, 'dp')
- feat_grad: float32 [7, 12288], P(None, 'dp')
The draws below stay inside these ranges and needn't reach their ends.
All inputs are finite; a program needn't handle non-finite values.
Results may differ from the reference program's by a relative error of at most 0.0041.
Values may be sent and summed in bfloat16 or wider, within the bound.
A program may use at most 128 MiB of HBM per device.

```python
import jax
import jax.numpy as jnp
from jax import lax

C = 4096
FEAT = 7
FILT = 128
TOKENS = 2048
SEQS = 2


def with_spikes(values, key, source, target, blocks, factor):
    def block_of(dim):
        return (jnp.arange(values.shape[dim]) // (values.shape[dim] // blocks)).reshape((-1,) + (1,) * (values.ndim - 1 - dim))

    first = jax.random.permutation(key, blocks)[block_of(target)]
    other_side = (block_of(target) + blocks // 2) % blocks
    return jnp.where((block_of(source) == first) | (block_of(source) == other_side), factor * values, values)


def levels(stream_key, dims, cuts, smallest, high):
    factor_of, own = 1.0, jax.random.fold_in(stream_key, 6)
    for dim, blocks in cuts:
        heights = jnp.exp(jax.random.uniform(jax.random.fold_in(own, dim), (blocks,), jnp.float32, smallest / len(cuts), high / len(cuts)))
        factor_of = factor_of * jnp.repeat(heights, dims[dim] // blocks).reshape([-1 if axis == dim else 1 for axis in range(len(dims))])
    return factor_of


def bell_draw(own_key, extent, spread, limit, pieces=(), kind=jnp.bfloat16):
    values = jax.random.normal(own_key, extent, jnp.float32) * spread
    if len(pieces) > 0:
        values = levels(own_key, extent, pieces, -0.22, 0.18) * values
    return jnp.clip(values, min=-limit, max=limit).astype(kind)


def noise_with(key, extent, width, most, split, heavy, kind=jnp.bfloat16):
    entries = width * jax.random.normal(key, extent, jnp.float32)
    if split:
        entries = entries * levels(key, extent, split, -0.22, 0.18)
    return jnp.clip(with_spikes(entries, jax.random.fold_in(key, 3), *heavy), -most, most).astype(kind)


def setup_inputs(seed: int = 0) -> dict:
    splits = jax.random.split(jax.random.key(seed), 5)
    inputs = bell_draw(splits[0], (SEQS, TOKENS, 3 * C), 1.0, 6.0, ((0, 2), (1, 16)))
    feat_weight = bell_draw(splits[1], (FEAT, 3 * C), FEAT ** -0.5, 2.0, ((1, 2),), jnp.float32)
    filter_taps = bell_draw(splits[2], (FILT, C), FILT ** -0.5, 0.5, ((1, 2),), jnp.float32)
    upstream = noise_with(splits[3], (SEQS, TOKENS, C), 1.0, 6.0, ((0, 2), (1, 16)), (0, 2, 2, 2.0))
    return dict(inputs=inputs, feat_weight=feat_weight, filter_taps=filter_taps, upstream=upstream)


def delayed(values, steps):
    if steps == 0:
        return values
    padding = jnp.zeros((steps,) + values.shape[1:], values.dtype)
    return jnp.concatenate([padding, values[:values.shape[0] - steps]], 0)


def sequence_terms(operands, feat_weight, filter_taps):
    signal, grad_out = operands
    signal_wide = signal.astype(jnp.float32)
    featured = sum(feat_weight[offset] * delayed(signal_wide, offset) for offset in range(FEAT))
    query = featured[:, :C]
    key_part = featured[:, C:2 * C]
    value_part = featured[:, 2 * C:]
    mixed = (key_part * value_part).astype(jnp.bfloat16)
    seq_length = signal.shape[0]
    padded = 2 * seq_length
    mixed_hat = jnp.fft.rfft(mixed.astype(jnp.float32), n=padded, axis=0)
    taps_hat = jnp.fft.rfft(filter_taps, n=padded, axis=0)
    conv_out = jnp.fft.irfft(mixed_hat * taps_hat, n=padded, axis=0)[:seq_length]
    grad_wide = grad_out.astype(jnp.float32)
    grad_conv = (grad_wide * query).astype(jnp.bfloat16)
    grad_hat = jnp.fft.rfft(grad_conv.astype(jnp.float32), n=padded, axis=0)
    grad_mixed = jnp.fft.irfft(grad_hat * jnp.conj(taps_hat), n=padded, axis=0)[:seq_length]
    filter_part = jnp.fft.irfft(grad_hat * jnp.conj(mixed_hat), n=padded, axis=0)[:FILT]
    grad_feat = jnp.concatenate([grad_wide * conv_out, grad_mixed * value_part, grad_mixed * key_part], 1)
    feat_part = jnp.stack([jnp.sum(grad_feat * delayed(signal_wide, offset), 0) for offset in range(FEAT)], 0)
    return filter_part, feat_part


def reference(inputs, feat_weight, filter_taps, upstream):
    parts = lax.map(lambda operands: sequence_terms(operands, feat_weight, filter_taps), (inputs, upstream))
    scale = (SEQS * TOKENS) ** -0.5
    return jnp.sum(parts[0], 0) * scale, jnp.sum(parts[1], 0) * scale
```

```python
import functools

import jax
import jax.numpy as jnp
import numpy as np
from jax import lax
from jax.experimental import pallas as pl
from jax.experimental.pallas import tpu as pltpu
from jax.sharding import PartitionSpec as P

PAD = 8
F32 = jnp.float32
BF16 = jnp.bfloat16


def from_behind(block, axis, distance):
    devices = range(lax.axis_size(axis))
    route = [(i - distance, i) for i in devices if i - distance in devices]
    return lax.ppermute(block, axis, route)


def two_parts(matrix):
    high = matrix.astype(BF16)
    low = (matrix - high.astype(np.float64)).astype(BF16)
    return high, low


def transforms(rows, taps):
    size = rows + taps
    half = size // 2
    angle = 2 * np.pi * np.outer(np.arange(half), np.arange(size)) / size
    cosines = np.cos(angle)
    sines = -np.sin(angle)
    sines[0] = np.cos(np.pi * np.arange(size))
    forward = np.concatenate([cosines, sines], 0)
    weight = np.full((size, 1), 2.0 / size)
    weight[0] = weight[half] = 1.0 / size
    backward = (forward * weight).T
    f_high, f_low = two_parts(forward)
    b_high, b_low = two_parts(backward)
    cat = lambda *parts: np.concatenate(parts, 1)
    return (
        cat(f_high[:, :rows], f_low[:, :rows]),
        cat(f_high[:, :taps], f_low[:, :taps], f_high[:, :taps]),
        cat(f_high, f_low),
        cat(b_high, b_low),
    )


def dot(a, b):
    return jnp.dot(a, b, preferred_element_type=F32)


def chunk_terms(q_ext, k_ext, v_ext, up_ext, taps, weights, mats, rows, reach):
    to_mixed, to_taps, to_grad, back = mats
    size = up_ext.shape[0]
    half = size // 2

    def featured(ext, w, out_rows):
        total = w[0:1] * ext[PAD : PAD + out_rows, :]
        for j in range(1, reach):
            total += w[j : j + 1] * ext[PAD - j : PAD - j + out_rows, :]
        return total

    def lagged(grad, ext, out_rows):
        sums = [
            jnp.sum(grad * ext[PAD - j : PAD - j + out_rows, :], 0, keepdims=True)
            for j in range(reach)
        ]
        sums += [jnp.zeros_like(sums[0])] * (PAD - reach)
        return jnp.concatenate(sums, 0)

    key_part = featured(k_ext, weights[1], rows)
    value_part = featured(v_ext, weights[2], rows)
    mixed = (key_part * value_part).astype(BF16)
    m_hat = dot(to_mixed[...], jnp.concatenate([mixed, mixed], 0))
    taps_high = taps.astype(BF16)
    taps_low = (taps - taps_high.astype(F32)).astype(BF16)
    t_hat = dot(to_taps[...], jnp.concatenate([taps_high, taps_high, taps_low], 0))
    query = featured(q_ext, weights[0], size)
    grad_conv = (up_ext[...].astype(F32) * query).astype(BF16)
    g_hat = dot(to_grad[...], jnp.concatenate([grad_conv, grad_conv], 0))

    m_re, m_im = m_hat[:half], m_hat[half:]
    t_re, t_im = t_hat[:half], t_hat[half:]
    g_re, g_im = g_hat[:half], g_hat[half:]
    first = lax.broadcasted_iota(jnp.int32, m_re.shape, 0) == 0
    t_imz = jnp.where(first, 0.0, t_im)
    t_ren = jnp.where(first, t_im, t_re)
    m_imz = jnp.where(first, 0.0, m_im)
    m_ren = jnp.where(first, m_im, m_re)

    def inverse(re, im, out_rows):
        re, im = re.astype(BF16), im.astype(BF16)
        return dot(back[:out_rows, :], jnp.concatenate([re, im, re, im], 0))

    conv_out = inverse(
        m_re * t_re - m_im * t_imz, m_re * t_imz + m_im * t_ren, size
    )
    grad_mixed = inverse(
        g_re * t_re + g_im * t_imz, g_im * t_ren - g_re * t_imz, rows
    )
    filter_part = inverse(
        g_re * m_re + g_im * m_imz, g_im * m_ren - g_re * m_imz, taps.shape[0]
    )
    return (
        filter_part,
        lagged(up_ext[...].astype(F32) * conv_out, q_ext, size),
        lagged(grad_mixed * value_part, k_ext, rows),
        lagged(grad_mixed * key_part, v_ext, rows),
    )


def local_kernel(
    reach, xq, xk, xv, pq, pk, pv, nq, up, nup, taps, wq, wk, wv, m0, m1, m2, m3,
    filt, fq, fk, fv, q_ext, k_ext, v_ext, up_ext,
):
    rows = xq.shape[0]
    size = up_ext.shape[0]
    for ext, prev, block in ((q_ext, pq, xq), (k_ext, pk, xk), (v_ext, pv, xv)):
        ext[0:PAD, :] = prev[...].astype(F32)
        ext[PAD : PAD + rows, :] = block[...].astype(F32)
    q_ext[PAD + rows : PAD + size, :] = nq[...].astype(F32)
    up_ext[0:rows, :] = up[...]
    up_ext[rows:size, :] = nup[...]
    filt[...], fq[...], fk[...], fv[...] = chunk_terms(
        q_ext, k_ext, v_ext, up_ext, taps[...], (wq[...], wk[...], wv[...]),
        (m0, m1, m2, m3), rows, reach,
    )


def per_device(inputs, feat_weight, filter_taps, upstream):
    inputs_here = inputs[0]
    grad_here = upstream[0]
    rows = inputs_here.shape[0]
    channels = grad_here.shape[1]
    filt_rows = filter_taps.shape[0]
    reach = feat_weight.shape[0]
    scale = (lax.axis_size("dp") * lax.axis_size("ctx") * rows) ** (-0.5)
    feat_full, taps_full = (
        lax.all_gather(feat_weight, "dp", axis=1, tiled=True),
        lax.all_gather(filter_taps, "dp", axis=1, tiled=True),
    )
    next_grad, next_query = from_behind(
        (grad_here[:filt_rows], inputs_here[:filt_rows, :channels]), "ctx", -1
    )
    before = from_behind(inputs_here[rows - PAD :], "ctx", 1)
    weights = jnp.concatenate(
        [feat_full, jnp.zeros((PAD - reach, feat_full.shape[1]), F32)], 0
    )
    mats = [jnp.asarray(m) for m in transforms(rows, filt_rows)]
    width = 256
    steps = channels // width
    size = rows + filt_rows
    part = lambda r, group: pl.BlockSpec((r, width), lambda i: (0, i + group * steps))
    whole = lambda m: pl.BlockSpec(m.shape, lambda i: (0, 0))
    out = lambda r: jax.ShapeDtypeStruct((r, channels), F32)
    filter_part, feat_q, feat_k, feat_v = pl.pallas_call(
        functools.partial(local_kernel, reach),
        grid=(steps,),
        out_shape=[out(filt_rows), out(PAD), out(PAD), out(PAD)],
        in_specs=[part(rows, g) for g in range(3)]
        + [part(PAD, g) for g in range(3)]
        + [part(filt_rows, 0), part(rows, 0), part(filt_rows, 0), part(filt_rows, 0)]
        + [part(PAD, g) for g in range(3)]
        + [whole(m) for m in mats],
        out_specs=[part(filt_rows, 0)] + [part(PAD, 0)] * 3,
        scratch_shapes=[
            pltpu.VMEM((PAD + size, width), F32),
            pltpu.VMEM((PAD + rows, width), F32),
            pltpu.VMEM((PAD + rows, width), F32),
            pltpu.VMEM((size, width), BF16),
        ],
    )(
        inputs_here, inputs_here, inputs_here, before, before, before, next_query,
        grad_here, next_grad, taps_full, weights, weights, weights, *mats,
    )
    feat_part = jnp.concatenate([feat_q, feat_k, feat_v], 1)[:reach]
    filter_summed, feat_summed = (
        lax.psum_scatter(filter_part, "dp", scatter_dimension=1, tiled=True),
        lax.psum_scatter(feat_part, "dp", scatter_dimension=1, tiled=True),
    )
    filter_whole, feat_whole = lax.psum((filter_summed, feat_summed), "ctx")
    return (filter_whole * scale, feat_whole * scale)


def solution(mesh):
    placed = (P("dp", "ctx", None), P(None, "dp"), P(None, "dp"), P("dp", "ctx", None))
    return jax.shard_map(
        per_device,
        mesh=mesh,
        in_specs=placed,
        out_specs=(P(None, "dp"), P(None, "dp")),
        check_vma=False,
    )
```

```python
import functools

import jax
import jax.numpy as jnp
import numpy as np
from jax import lax
from jax.experimental import pallas as pl
from jax.experimental.pallas import tpu as pltpu
from jax.sharding import PartitionSpec as P

PAD = 8
F32 = jnp.float32
BF16 = jnp.bfloat16


def from_behind(block, axis, distance):
    devices = range(lax.axis_size(axis))
    route = [(i - distance, i) for i in devices if i - distance in devices]
    return lax.ppermute(block, axis, route)


def two_parts(matrix):
    high = matrix.astype(BF16)
    low = (matrix - high.astype(np.float64)).astype(BF16)
    return high, low


def transforms(rows, taps):
    size = rows + taps
    half = size // 2
    angle = 2 * np.pi * np.outer(np.arange(half), np.arange(size)) / size
    cosines = np.cos(angle)
    sines = -np.sin(angle)
    sines[0] = np.cos(np.pi * np.arange(size))
    forward = np.concatenate([cosines, sines], 0)
    weight = np.full((size, 1), 2.0 / size)
    weight[0] = weight[half] = 1.0 / size
    backward = (forward * weight).T
    f_high, f_low = two_parts(forward)
    b_high, b_low = two_parts(backward)
    cat = lambda *parts: np.concatenate(parts, 1)
    return (
        cat(f_high[:, :rows], f_low[:, :rows]),
        cat(f_high[:, :taps], f_low[:, :taps], f_high[:, :taps]),
        cat(f_high, f_low),
        cat(b_high, b_low),
    )


def dot(a, b):
    return jnp.dot(a, b, preferred_element_type=F32)


def chunk_terms(q_ext, k_ext, v_ext, up_ext, taps, weights, mats, rows, reach):
    to_mixed, to_taps, to_grad, back = mats
    size = up_ext.shape[0]
    half = size // 2

    def featured(ext, w, out_rows):
        total = w[0:1] * ext[PAD : PAD + out_rows, :]
        for j in range(1, reach):
            total += w[j : j + 1] * ext[PAD - j : PAD - j + out_rows, :]
        return total

    def lagged(grad, ext, out_rows):
        sums = [
            jnp.sum(grad * ext[PAD - j : PAD - j + out_rows, :], 0, keepdims=True)
            for j in range(reach)
        ]
        sums += [jnp.zeros_like(sums[0])] * (PAD - reach)
        return jnp.concatenate(sums, 0)

    key_part = featured(k_ext, weights[1], rows)
    value_part = featured(v_ext, weights[2], rows)
    mixed = (key_part * value_part).astype(BF16)
    m_hat = dot(to_mixed[...], jnp.concatenate([mixed, mixed], 0))
    taps_high = taps.astype(BF16)
    taps_low = (taps - taps_high.astype(F32)).astype(BF16)
    t_hat = dot(to_taps[...], jnp.concatenate([taps_high, taps_high, taps_low], 0))
    query = featured(q_ext, weights[0], size)
    grad_conv = (up_ext[...].astype(F32) * query).astype(BF16)
    g_hat = dot(to_grad[...], jnp.concatenate([grad_conv, grad_conv], 0))

    m_re, m_im = m_hat[:half], m_hat[half:]
    t_re, t_im = t_hat[:half], t_hat[half:]
    g_re, g_im = g_hat[:half], g_hat[half:]
    first = lax.broadcasted_iota(jnp.int32, m_re.shape, 0) == 0
    t_imz = jnp.where(first, 0.0, t_im)
    t_ren = jnp.where(first, t_im, t_re)
    m_imz = jnp.where(first, 0.0, m_im)
    m_ren = jnp.where(first, m_im, m_re)

    def inverse(re, im, out_rows):
        re, im = re.astype(BF16), im.astype(BF16)
        return dot(back[:out_rows, :], jnp.concatenate([re, im, re, im], 0))

    conv_out = inverse(
        m_re * t_re - m_im * t_imz, m_re * t_imz + m_im * t_ren, size
    )
    grad_mixed = inverse(
        g_re * t_re + g_im * t_imz, g_im * t_ren - g_re * t_imz, rows
    )
    filter_part = inverse(
        g_re * m_re + g_im * m_imz, g_im * m_ren - g_re * m_imz, taps.shape[0]
    )
    return (
        filter_part,
        lagged(up_ext[...].astype(F32) * conv_out, q_ext, size),
        lagged(grad_mixed * value_part, k_ext, rows),
        lagged(grad_mixed * key_part, v_ext, rows),
    )


def local_kernel(
    reach, xq, xk, xv, pq, pk, pv, nq, up, nup, taps, wq, wk, wv, m0, m1, m2, m3,
    filt, fq, fk, fv, q_ext, k_ext, v_ext, up_ext,
):
    rows = xq.shape[0]
    size = up_ext.shape[0]
    for ext, prev, block in ((q_ext, pq, xq), (k_ext, pk, xk), (v_ext, pv, xv)):
        ext[0:PAD, :] = prev[...].astype(F32)
        ext[PAD : PAD + rows, :] = block[...].astype(F32)
    q_ext[PAD + rows : PAD + size, :] = nq[...].astype(F32)
    up_ext[0:rows, :] = up[...]
    up_ext[rows:size, :] = nup[...]
    filt[...], fq[...], fk[...], fv[...] = chunk_terms(
        q_ext, k_ext, v_ext, up_ext, taps[...], (wq[...], wk[...], wv[...]),
        (m0, m1, m2, m3), rows, reach,
    )


def by_collectives(inputs, feat_weight, filter_taps, upstream):
    inputs_here = inputs[0]
    grad_here = upstream[0]
    rows = inputs_here.shape[0]
    channels = grad_here.shape[1]
    filt_rows = filter_taps.shape[0]
    reach = feat_weight.shape[0]
    scale = (lax.axis_size("dp") * lax.axis_size("ctx") * rows) ** (-0.5)
    feat_full, taps_full = (
        lax.all_gather(feat_weight, "dp", axis=1, tiled=True),
        lax.all_gather(filter_taps, "dp", axis=1, tiled=True),
    )
    next_grad, next_query = from_behind(
        (grad_here[:filt_rows], inputs_here[:filt_rows, :channels]), "ctx", -1
    )
    before = from_behind(inputs_here[rows - PAD :], "ctx", 1)
    weights = jnp.concatenate(
        [feat_full, jnp.zeros((PAD - reach, feat_full.shape[1]), F32)], 0
    )
    mats = [jnp.asarray(m) for m in transforms(rows, filt_rows)]
    width = 256
    steps = channels // width
    size = rows + filt_rows
    part = lambda r, group: pl.BlockSpec((r, width), lambda i: (0, i + group * steps))
    whole = lambda m: pl.BlockSpec(m.shape, lambda i: (0, 0))
    out = lambda r: jax.ShapeDtypeStruct((r, channels), F32)
    filter_part, feat_q, feat_k, feat_v = pl.pallas_call(
        functools.partial(local_kernel, reach),
        grid=(steps,),
        out_shape=[out(filt_rows), out(PAD), out(PAD), out(PAD)],
        in_specs=[part(rows, g) for g in range(3)]
        + [part(PAD, g) for g in range(3)]
        + [part(filt_rows, 0), part(rows, 0), part(filt_rows, 0), part(filt_rows, 0)]
        + [part(PAD, g) for g in range(3)]
        + [whole(m) for m in mats],
        out_specs=[part(filt_rows, 0)] + [part(PAD, 0)] * 3,
        scratch_shapes=[
            pltpu.VMEM((PAD + size, width), F32),
            pltpu.VMEM((PAD + rows, width), F32),
            pltpu.VMEM((PAD + rows, width), F32),
            pltpu.VMEM((size, width), BF16),
        ],
    )(
        inputs_here, inputs_here, inputs_here, before, before, before, next_query,
        grad_here, next_grad, taps_full, weights, weights, weights, *mats,
    )
    feat_part = jnp.concatenate([feat_q, feat_k, feat_v], 1)[:reach]
    filter_summed, feat_summed = (
        lax.psum_scatter(filter_part, "dp", scatter_dimension=1, tiled=True),
        lax.psum_scatter(feat_part, "dp", scatter_dimension=1, tiled=True),
    )
    filter_whole, feat_whole = lax.psum((filter_summed, feat_summed), "ctx")
    return (filter_whole * scale, feat_whole * scale)


MESH = pl.DeviceIdType.MESH
LANES = 128


def fused_kernel(
    reach, scale, x, up, tail, taps_here, w_here, m0, m1, m2, m3, filt_out, feat_out,
    taps_all, w_all, prev, n_up, n_q, q_ext, k_ext, v_ext, up_ext,
    stage, dp_got, rs_send, rs_got, gathered,
    own_sem, swap_send, swap_got, tail_send, tail_got, halo_send, halo_got,
    dp_send, dp_recv, rs_ssem, rs_rsem, ag_ssem, ag_rsem,
):
    n = lax.axis_size("ctx")
    me, core = lax.axis_index("ctx"), lax.axis_index("dp")
    rows, filt_rows = x.shape[0], taps_here.shape[0]
    channels = up.shape[1]
    half = channels // 2
    feat_half = w_here.shape[1]
    size = rows + filt_rows
    packed = stage.shape[2]
    partner = {"dp": 1 - core}

    barrier = pltpu.get_barrier_semaphore()
    pl.semaphore_signal(barrier, inc=1, device_id=partner, device_id_type=MESH)

    @pl.loop(1, n)
    def _(j):
        pl.semaphore_signal(
            barrier, inc=1, device_id={"ctx": lax.rem(me + j, n)}, device_id_type=MESH
        )

    def remote(src, dst, send, got, device):
        return pltpu.make_async_remote_copy(
            src_ref=src, dst_ref=dst, send_sem=send, recv_sem=got,
            device_id=device, device_id_type=MESH,
        )

    def lanes_of(owner, piece):
        return pl.ds(pl.multiple_of(owner * LANES + piece * half, LANES), LANES)

    def swaps():
        taps_side = pl.ds(pl.multiple_of(core * half, LANES), half)
        feat_side = pl.ds(pl.multiple_of(core * feat_half, LANES), feat_half)
        return (
            remote(taps_here, taps_all.at[:, taps_side], swap_send.at[0], swap_got.at[0], partner),
            remote(w_here, w_all.at[:, feat_side], swap_send.at[1], swap_got.at[1], partner),
        ), (
            pltpu.make_async_copy(taps_here, taps_all.at[:, taps_side], own_sem.at[0]),
            pltpu.make_async_copy(w_here, w_all.at[:, feat_side], own_sem.at[1]),
        )

    def tail_copy():
        return remote(tail, prev, tail_send, tail_got, {"ctx": lax.rem(me + 1, n)})

    def halo_copies(i, owner):
        target = {"ctx": lax.rem(me + n - 1, n)}
        copies = []
        for piece in range(2):
            at = lanes_of(owner, piece)
            for k, (src, dst) in enumerate(((up, n_up), (x, n_q))):
                s = 2 * piece + k
                copies.append(
                    remote(
                        src.at[pl.ds(0, filt_rows), at], dst.at[:, at],
                        halo_send.at[i, s], halo_got.at[i, s], target,
                    )
                )
        return copies

    sent, kept = swaps()
    for copy in kept:
        copy.start()

    @pl.when(me == 0)
    def _():
        prev[...] = jnp.zeros_like(prev)

    @pl.when(me == n - 1)
    def _():
        n_up[...] = jnp.zeros_like(n_up)
        n_q[...] = jnp.zeros_like(n_q)

    pl.semaphore_wait(barrier, n)
    for copy in sent:
        copy.start()

    @pl.when(me < n - 1)
    def _():
        tail_copy().start()

    @pl.when(me > 0)
    def _():
        @pl.loop(0, n)
        def _(i):
            for copy in halo_copies(i, lax.rem(i + me, n)):
                copy.start()

    for copy in kept:
        copy.wait()
    for copy in sent:
        copy.wait()

    @pl.when(me > 0)
    def _():
        tail_copy().wait_recv()

    def dp_copy(i):
        return remote(
            stage.at[i, 1 - core], dp_got.at[i], dp_send.at[i], dp_recv.at[i], partner
        )

    def rs_copy(i, owner):
        return remote(
            rs_send.at[i], rs_got.at[me], rs_ssem.at[i], rs_rsem.at[me], {"ctx": owner}
        )

    def owner_at(i):
        return lax.rem(i + 1 + me, n)

    def compute(i):
        owner = owner_at(i)

        @pl.when(me < n - 1)
        def _():
            for copy in halo_copies(i, owner):
                copy.wait_recv()

        def both(ref, group):
            return jnp.concatenate(
                [ref[:, pl.ds(pl.multiple_of(group * channels + p * half + owner * LANES, LANES), LANES)] for p in range(2)],
                1,
            )

        for group, ext in enumerate((q_ext, k_ext, v_ext)):
            ext[0:PAD, :] = both(prev, group).astype(F32)
            ext[PAD : PAD + rows, :] = both(x, group).astype(F32)
        q_ext[PAD + rows : PAD + size, :] = both(n_q, 0).astype(F32)
        up_ext[0:rows, :] = both(up, 0)
        up_ext[rows:size, :] = both(n_up, 0)
        filt, feat_q, feat_k, feat_v = chunk_terms(
            q_ext, k_ext, v_ext, up_ext, both(taps_all, 0),
            [both(w_all, group) for group in range(3)],
            (m0, m1, m2, m3), rows, reach,
        )
        a, b = slice(0, LANES), slice(LANES, 2 * LANES)
        rest = [jnp.zeros((packed - filt_rows - 3 * PAD, LANES), F32)]
        stage[i, 0] = jnp.concatenate(
            [filt[:, a], feat_q[:, a], feat_q[:, b], feat_k[:, a]] + rest, 0
        )
        stage[i, 1] = jnp.concatenate(
            [filt[:, b], feat_k[:, b], feat_v[:, a], feat_v[:, b]] + rest, 0
        )
        dp_copy(i).start()

    def reduce_pair(i):
        dp_copy(i).wait_recv()
        return (stage[i, core] + dp_got[i]).astype(BF16)

    def send_on(i):
        rs_send[i] = reduce_pair(i)
        rs_copy(i, owner_at(i)).start()

    @pl.loop(0, n)
    def _(i):
        compute(i)

        @pl.when(i > 0)
        def _():
            send_on(i - 1)

    total = reduce_pair(n - 1).astype(F32)
    for j in range(1, n):
        src = lax.rem(me + j, n)
        remote(
            rs_send.at[0], rs_got.at[src], rs_ssem.at[0], rs_rsem.at[src], {"ctx": src}
        ).wait_recv()
        total += rs_got[src].astype(F32)
    gathered[me] = total.astype(BF16)

    def ag_copy(owner, target):
        return remote(
            gathered.at[owner], gathered.at[owner], ag_ssem.at[target], ag_rsem.at[owner],
            {"ctx": target},
        )

    @pl.loop(1, n)
    def _(j):
        ag_copy(me, lax.rem(me + j, n)).start()

    def unpack(owner):
        value = gathered[owner].astype(F32) * scale
        filt_out[:, pl.ds(pl.multiple_of(owner * LANES, LANES), LANES)] = value[:filt_rows]
        for g in range(3):
            low = filt_rows + g * PAD
            at = pl.ds(pl.multiple_of(owner * LANES + g * half, LANES), LANES)
            feat_out[:, at] = value[low : low + reach]

    unpack(me)

    @pl.loop(1, n)
    def _(j):
        src = lax.rem(me + j, n)
        ag_copy(src, src).wait_recv()
        unpack(src)

    @pl.when(me < n - 1)
    def _():
        tail_copy().wait_send()

    @pl.when(me > 0)
    def _():
        @pl.loop(0, n)
        def _(i):
            for copy in halo_copies(i, lax.rem(i + me, n)):
                copy.wait_send()

    @pl.loop(0, n)
    def _(i):
        dp_copy(i).wait_send()

    @pl.loop(0, n - 1)
    def _(i):
        rs_copy(i, owner_at(i)).wait_send()

    @pl.loop(1, n)
    def _(j):
        ag_copy(me, lax.rem(me + j, n)).wait_send()


def fused(inputs, feat_weight, filter_taps, upstream):
    x, up = inputs[0], upstream[0]
    n = lax.axis_size("ctx")
    rows, channels = up.shape
    filt_rows, reach = filter_taps.shape[0], feat_weight.shape[0]
    scale = (lax.axis_size("dp") * n * rows) ** (-0.5)
    mats = [jnp.asarray(m) for m in transforms(rows, filt_rows)]
    size = rows + filt_rows
    width = 2 * LANES
    packed = -(-(filt_rows + 3 * PAD) // 16) * 16
    dma = lambda *shape: pltpu.SemaphoreType.DMA(shape)
    return pl.pallas_call(
        functools.partial(fused_kernel, reach, scale),
        out_shape=[
            jax.ShapeDtypeStruct(filter_taps.shape, F32),
            jax.ShapeDtypeStruct(feat_weight.shape, F32),
        ],
        in_specs=[pl.BlockSpec(memory_space=pltpu.VMEM)] * 9,
        out_specs=[pl.BlockSpec(memory_space=pltpu.VMEM)] * 2,
        scratch_shapes=[
            pltpu.VMEM((filt_rows, channels), F32),
            pltpu.VMEM((reach, x.shape[1]), F32),
            pltpu.VMEM((PAD, x.shape[1]), BF16),
            pltpu.VMEM((filt_rows, channels), BF16),
            pltpu.VMEM((filt_rows, channels), BF16),
            pltpu.VMEM((PAD + size, width), F32),
            pltpu.VMEM((PAD + rows, width), F32),
            pltpu.VMEM((PAD + rows, width), F32),
            pltpu.VMEM((size, width), BF16),
            pltpu.VMEM((n, 2, packed, LANES), F32),
            pltpu.VMEM((n, packed, LANES), F32),
            pltpu.VMEM((n, packed, LANES), BF16),
            pltpu.VMEM((n, packed, LANES), BF16),
            pltpu.VMEM((n, packed, LANES), BF16),
            dma(2), dma(2), dma(2),
            pltpu.SemaphoreType.DMA, pltpu.SemaphoreType.DMA,
            dma(n, 4), dma(n, 4),
            dma(n), dma(n), dma(n), dma(n), dma(n), dma(n),
        ],
        compiler_params=pltpu.CompilerParams(
            collective_id=0, has_side_effects=True, vmem_limit_bytes=60 * 2**20
        ),
    )(x, up, x[rows - PAD :], filter_taps, feat_weight, *mats)


def per_device(inputs, feat_weight, filter_taps, upstream):
    cut = 2 * lax.axis_size("ctx") * LANES
    if lax.axis_size("dp") == 2 and upstream.shape[2] == cut:
        return fused(inputs, feat_weight, filter_taps, upstream)
    return by_collectives(inputs, feat_weight, filter_taps, upstream)


def solution(mesh):
    placed = (P("dp", "ctx", None), P(None, "dp"), P(None, "dp"), P("dp", "ctx", None))
    return jax.shard_map(
        per_device,
        mesh=mesh,
        in_specs=placed,
        out_specs=(P(None, "dp"), P(None, "dp")),
        check_vma=False,
    )
```

```python
import functools

import jax
import jax.numpy as jnp
import numpy as np
from jax import lax
from jax.experimental import pallas as pl
from jax.experimental.pallas import tpu as pltpu
from jax.sharding import PartitionSpec as P

PAD = 8
F32 = jnp.float32
BF16 = jnp.bfloat16


def from_behind(block, axis, distance):
    devices = range(lax.axis_size(axis))
    route = [(i - distance, i) for i in devices if i - distance in devices]
    return lax.ppermute(block, axis, route)


def two_parts(matrix):
    high = matrix.astype(BF16)
    low = (matrix - high.astype(np.float64)).astype(BF16)
    return high, low


def transforms(rows, taps):
    size = rows + taps
    half = size // 2
    angle = 2 * np.pi * np.outer(np.arange(half), np.arange(size)) / size
    cosines = np.cos(angle)
    sines = -np.sin(angle)
    sines[0] = np.cos(np.pi * np.arange(size))
    forward = np.concatenate([cosines, sines], 0)
    weight = np.full((size, 1), 2.0 / size)
    weight[0] = weight[half] = 1.0 / size
    backward = (forward * weight).T
    f_high, f_low = two_parts(forward)
    b_high, b_low = two_parts(backward)
    cat = lambda *parts: np.concatenate(parts, 1)
    return (
        cat(f_high[:, :rows], f_low[:, :rows]),
        cat(f_high[:, :taps], f_low[:, :taps], f_high[:, :taps]),
        cat(f_high, f_low),
        cat(b_high, b_low),
    )


def dot(a, b):
    return jnp.dot(a, b, preferred_element_type=F32)


def chunk_terms(q_ext, k_ext, v_ext, up_ext, taps, weights, mats, rows, reach):
    to_mixed, to_taps, to_grad, back = mats
    size = up_ext.shape[0]
    half = size // 2

    def featured(ext, w, out_rows):
        total = w[0:1] * ext[PAD : PAD + out_rows, :]
        for j in range(1, reach):
            total += w[j : j + 1] * ext[PAD - j : PAD - j + out_rows, :]
        return total

    def lagged(grad, ext, out_rows):
        sums = [
            jnp.sum(grad * ext[PAD - j : PAD - j + out_rows, :], 0, keepdims=True)
            for j in range(reach)
        ]
        sums += [jnp.zeros_like(sums[0])] * (PAD - reach)
        return jnp.concatenate(sums, 0)

    key_part = featured(k_ext, weights[1], rows)
    value_part = featured(v_ext, weights[2], rows)
    mixed = (key_part * value_part).astype(BF16)
    m_hat = dot(to_mixed[...], jnp.concatenate([mixed, mixed], 0))
    taps_high = taps.astype(BF16)
    taps_low = (taps - taps_high.astype(F32)).astype(BF16)
    t_hat = dot(to_taps[...], jnp.concatenate([taps_high, taps_high, taps_low], 0))
    query = featured(q_ext, weights[0], size)
    grad_conv = (up_ext[...].astype(F32) * query).astype(BF16)
    g_hat = dot(to_grad[...], jnp.concatenate([grad_conv, grad_conv], 0))

    m_re, m_im = m_hat[:half], m_hat[half:]
    t_re, t_im = t_hat[:half], t_hat[half:]
    g_re, g_im = g_hat[:half], g_hat[half:]
    first = lax.broadcasted_iota(jnp.int32, m_re.shape, 0) == 0
    t_imz = jnp.where(first, 0.0, t_im)
    t_ren = jnp.where(first, t_im, t_re)
    m_imz = jnp.where(first, 0.0, m_im)
    m_ren = jnp.where(first, m_im, m_re)

    def inverse(re, im, out_rows):
        re, im = re.astype(BF16), im.astype(BF16)
        return dot(back[:out_rows, :], jnp.concatenate([re, im, re, im], 0))

    conv_out = inverse(
        m_re * t_re - m_im * t_imz, m_re * t_imz + m_im * t_ren, size
    )
    grad_mixed = inverse(
        g_re * t_re + g_im * t_imz, g_im * t_ren - g_re * t_imz, rows
    )
    filter_part = inverse(
        g_re * m_re + g_im * m_imz, g_im * m_ren - g_re * m_imz, taps.shape[0]
    )
    return (
        filter_part,
        lagged(up_ext[...].astype(F32) * conv_out, q_ext, size),
        lagged(grad_mixed * value_part, k_ext, rows),
        lagged(grad_mixed * key_part, v_ext, rows),
    )


def local_kernel(
    reach, xq, xk, xv, pq, pk, pv, nq, up, nup, taps, wq, wk, wv, m0, m1, m2, m3,
    filt, fq, fk, fv, q_ext, k_ext, v_ext, up_ext,
):
    rows = xq.shape[0]
    size = up_ext.shape[0]
    for ext, prev, block in ((q_ext, pq, xq), (k_ext, pk, xk), (v_ext, pv, xv)):
        ext[0:PAD, :] = prev[...].astype(F32)
        ext[PAD : PAD + rows, :] = block[...].astype(F32)
    q_ext[PAD + rows : PAD + size, :] = nq[...].astype(F32)
    up_ext[0:rows, :] = up[...]
    up_ext[rows:size, :] = nup[...]
    filt[...], fq[...], fk[...], fv[...] = chunk_terms(
        q_ext, k_ext, v_ext, up_ext, taps[...], (wq[...], wk[...], wv[...]),
        (m0, m1, m2, m3), rows, reach,
    )


def by_collectives(inputs, feat_weight, filter_taps, upstream):
    inputs_here = inputs[0]
    grad_here = upstream[0]
    rows = inputs_here.shape[0]
    channels = grad_here.shape[1]
    filt_rows = filter_taps.shape[0]
    reach = feat_weight.shape[0]
    scale = (lax.axis_size("dp") * lax.axis_size("ctx") * rows) ** (-0.5)
    feat_full, taps_full = (
        lax.all_gather(feat_weight, "dp", axis=1, tiled=True),
        lax.all_gather(filter_taps, "dp", axis=1, tiled=True),
    )
    next_grad, next_query = from_behind(
        (grad_here[:filt_rows], inputs_here[:filt_rows, :channels]), "ctx", -1
    )
    before = from_behind(inputs_here[rows - PAD :], "ctx", 1)
    weights = jnp.concatenate(
        [feat_full, jnp.zeros((PAD - reach, feat_full.shape[1]), F32)], 0
    )
    mats = [jnp.asarray(m) for m in transforms(rows, filt_rows)]
    width = 256
    steps = channels // width
    size = rows + filt_rows
    part = lambda r, group: pl.BlockSpec((r, width), lambda i: (0, i + group * steps))
    whole = lambda m: pl.BlockSpec(m.shape, lambda i: (0, 0))
    out = lambda r: jax.ShapeDtypeStruct((r, channels), F32)
    filter_part, feat_q, feat_k, feat_v = pl.pallas_call(
        functools.partial(local_kernel, reach),
        grid=(steps,),
        out_shape=[out(filt_rows), out(PAD), out(PAD), out(PAD)],
        in_specs=[part(rows, g) for g in range(3)]
        + [part(PAD, g) for g in range(3)]
        + [part(filt_rows, 0), part(rows, 0), part(filt_rows, 0), part(filt_rows, 0)]
        + [part(PAD, g) for g in range(3)]
        + [whole(m) for m in mats],
        out_specs=[part(filt_rows, 0)] + [part(PAD, 0)] * 3,
        scratch_shapes=[
            pltpu.VMEM((PAD + size, width), F32),
            pltpu.VMEM((PAD + rows, width), F32),
            pltpu.VMEM((PAD + rows, width), F32),
            pltpu.VMEM((size, width), BF16),
        ],
    )(
        inputs_here, inputs_here, inputs_here, before, before, before, next_query,
        grad_here, next_grad, taps_full, weights, weights, weights, *mats,
    )
    feat_part = jnp.concatenate([feat_q, feat_k, feat_v], 1)[:reach]
    filter_summed, feat_summed = (
        lax.psum_scatter(filter_part, "dp", scatter_dimension=1, tiled=True),
        lax.psum_scatter(feat_part, "dp", scatter_dimension=1, tiled=True),
    )
    filter_whole, feat_whole = lax.psum((filter_summed, feat_summed), "ctx")
    return (filter_whole * scale, feat_whole * scale)


MESH = pl.DeviceIdType.MESH
LANES = 128
GROUP = 2
PLANE = 4


def fused_kernel(
    reach, scale, x, up, taps_here, w_here, m0, m1, m2, m3, filt_out, feat_out,
    taps_all, w_all, tail, prev, n_up, n_q, r_up, r_q, q_ext, k_ext, v_ext, up_ext,
    stage, dp_got, rs_send, rs_got, gathered,
    own_sem, swap_send, swap_got, tail_send, tail_got, halo_send, halo_got,
    relay_send, relay_got,
    dp_send, dp_recv, rs_ssem, rs_rsem, ag_ssem, ag_rsem,
):
    n = lax.axis_size("ctx")
    me, core = lax.axis_index("ctx"), lax.axis_index("dp")
    rows, filt_rows = x.shape[0], taps_here.shape[0]
    channels = up.shape[1]
    half = channels // 2
    feat_half = w_here.shape[1]
    size = rows + filt_rows
    packed = stage.shape[2]
    partner = {"dp": 1 - core}

    barrier = pltpu.get_barrier_semaphore()
    pl.semaphore_signal(barrier, inc=1, device_id=partner, device_id_type=MESH)

    @pl.loop(1, n)
    def _(j):
        pl.semaphore_signal(
            barrier, inc=1, device_id={"ctx": lax.rem(me + j, n)}, device_id_type=MESH
        )

    def remote(src, dst, send, got, device):
        return pltpu.make_async_remote_copy(
            src_ref=src, dst_ref=dst, send_sem=send, recv_sem=got,
            device_id=device, device_id_type=MESH,
        )

    def lanes_of(owner, piece):
        return pl.ds(pl.multiple_of(owner * LANES + piece * half, LANES), LANES)

    def swaps():
        taps_side = pl.ds(pl.multiple_of(core * half, LANES), half)
        feat_side = pl.ds(pl.multiple_of(core * feat_half, LANES), feat_half)
        return (
            remote(taps_here, taps_all.at[:, taps_side], swap_send.at[0], swap_got.at[0], partner),
            remote(w_here, w_all.at[:, feat_side], swap_send.at[1], swap_got.at[1], partner),
        ), (
            pltpu.make_async_copy(taps_here, taps_all.at[:, taps_side], own_sem.at[0]),
            pltpu.make_async_copy(w_here, w_all.at[:, feat_side], own_sem.at[1]),
        )

    def tail_copy():
        return remote(tail, prev, tail_send, tail_got, {"ctx": lax.rem(me + 1, n)})

    groups = n // GROUP

    def block_copies(g, first, sources, targets, send, got, device):
        copies = []
        for piece in range(2):
            low = first * (GROUP * LANES) + piece * half
            at = pl.ds(pl.multiple_of(low, LANES), GROUP * LANES)
            for k, (src, dst) in enumerate(zip(sources, targets)):
                s = 2 * piece + k
                copies.append(
                    remote(
                        src.at[pl.ds(0, filt_rows), at], dst.at[:, at],
                        send.at[g, s], got.at[g, s], {"ctx": device},
                    )
                )
        return copies

    head, landing, relay = (up, x), (n_up, n_q), (r_up, r_q)
    near = (me > 0) & (lax.rem(me, PLANE) != 0)
    far = (me > 0) & (lax.rem(me, PLANE) == 0)
    relays = (lax.rem(me, PLANE) == 0) & (me < n - PLANE)

    def near_copies(g):
        back = lax.rem(me + n - 1, n)
        return block_copies(
            g, group_at(g, back), head, landing, halo_send, halo_got, back
        )

    def far_copies(g):
        back = lax.rem(me + n - 1, n)
        via = lax.rem(me + n - PLANE, n)
        return block_copies(g, group_at(g, back), head, relay, halo_send, relay_got, via)

    def arrivals(g):
        return block_copies(
            g, group_at(g, me), head, landing, halo_send, halo_got, lax.rem(me + 1, n)
        )

    def relay_arrivals(g):
        end = lax.rem(me + PLANE - 1, n)
        return block_copies(
            g, group_at(g, end), head, relay, halo_send, relay_got, lax.rem(me + PLANE, n)
        )

    def relay_copies(g):
        end = lax.rem(me + PLANE - 1, n)
        return block_copies(
            g, group_at(g, end), relay, landing, relay_send, halo_got, end
        )

    def group_at(g, device):
        return lax.rem(g + 1 + device // GROUP, groups)

    sent, kept = swaps()
    for copy in kept:
        copy.start()

    tail[...] = x[rows - PAD :, :]

    @pl.when(me == 0)
    def _():
        prev[...] = jnp.zeros_like(prev)

    @pl.when(me == n - 1)
    def _():
        n_up[...] = jnp.zeros_like(n_up)
        n_q[...] = jnp.zeros_like(n_q)

    pl.semaphore_wait(barrier, n)
    for copy in sent:
        copy.start()

    @pl.when(me < n - 1)
    def _():
        tail_copy().start()

    @pl.when(near)
    def _():
        @pl.loop(0, groups)
        def _(g):
            for copy in near_copies(g):
                copy.start()

    @pl.when(far)
    def _():
        @pl.loop(0, groups)
        def _(g):
            for copy in far_copies(g):
                copy.start()

    for copy in kept:
        copy.wait()
    for copy in sent:
        copy.wait()

    @pl.when(me > 0)
    def _():
        tail_copy().wait_recv()

    def dp_copy(i):
        return remote(
            stage.at[i, 1 - core], dp_got.at[i], dp_send.at[i], dp_recv.at[i], partner
        )

    def rs_copy(i, owner):
        return remote(
            rs_send.at[i], rs_got.at[me], rs_ssem.at[i], rs_rsem.at[me], {"ctx": owner}
        )

    def owner_at(i):
        return group_at(i // GROUP, me) * GROUP + lax.rem(i + 1 + me, GROUP)

    def compute(i):
        owner = owner_at(i)

        @pl.when(relays & (lax.rem(i, GROUP) == 0))
        def _():
            g = i // GROUP
            for came, goes in zip(relay_arrivals(g), relay_copies(g)):
                came.wait_recv()
                goes.start()

        @pl.when((me < n - 1) & (lax.rem(i, GROUP) == 0))
        def _():
            for copy in arrivals(i // GROUP):
                copy.wait_recv()

        def both(ref, group):
            return jnp.concatenate(
                [ref[:, pl.ds(pl.multiple_of(group * channels + p * half + owner * LANES, LANES), LANES)] for p in range(2)],
                1,
            )

        for group, ext in enumerate((q_ext, k_ext, v_ext)):
            ext[0:PAD, :] = both(prev, group).astype(F32)
            ext[PAD : PAD + rows, :] = both(x, group).astype(F32)
        q_ext[PAD + rows : PAD + size, :] = both(n_q, 0).astype(F32)
        up_ext[0:rows, :] = both(up, 0)
        up_ext[rows:size, :] = both(n_up, 0)
        filt, feat_q, feat_k, feat_v = chunk_terms(
            q_ext, k_ext, v_ext, up_ext, both(taps_all, 0),
            [both(w_all, group) for group in range(3)],
            (m0, m1, m2, m3), rows, reach,
        )
        a, b = slice(0, LANES), slice(LANES, 2 * LANES)
        rest = [jnp.zeros((packed - filt_rows - 3 * PAD, LANES), F32)]
        stage[i, 0] = jnp.concatenate(
            [filt[:, a], feat_q[:, a], feat_q[:, b], feat_k[:, a]] + rest, 0
        )
        stage[i, 1] = jnp.concatenate(
            [filt[:, b], feat_k[:, b], feat_v[:, a], feat_v[:, b]] + rest, 0
        )
        dp_copy(i).start()

    def reduce_pair(i):
        dp_copy(i).wait_recv()
        return (stage[i, core] + dp_got[i]).astype(BF16)

    def send_on(i):
        rs_send[i] = reduce_pair(i)
        rs_copy(i, owner_at(i)).start()

    @pl.loop(0, n)
    def _(i):
        compute(i)

        @pl.when(i > 0)
        def _():
            send_on(i - 1)

    total = reduce_pair(n - 1).astype(F32)
    for j in range(1, n):
        src = lax.rem(me + j, n)
        remote(
            rs_send.at[0], rs_got.at[src], rs_ssem.at[0], rs_rsem.at[src], {"ctx": src}
        ).wait_recv()
        total += rs_got[src].astype(F32)
    gathered[me] = total.astype(BF16)

    def ag_copy(owner, target):
        return remote(
            gathered.at[owner], gathered.at[owner], ag_ssem.at[target], ag_rsem.at[owner],
            {"ctx": target},
        )

    @pl.loop(1, n)
    def _(j):
        ag_copy(me, lax.rem(me + j, n)).start()

    def unpack(owner):
        value = gathered[owner].astype(F32) * scale
        filt_out[:, pl.ds(pl.multiple_of(owner * LANES, LANES), LANES)] = value[:filt_rows]
        for g in range(3):
            low = filt_rows + g * PAD
            at = pl.ds(pl.multiple_of(owner * LANES + g * half, LANES), LANES)
            feat_out[:, at] = value[low : low + reach]

    unpack(me)

    @pl.loop(1, n)
    def _(j):
        src = lax.rem(me + j, n)
        ag_copy(src, src).wait_recv()
        unpack(src)

    @pl.when(me < n - 1)
    def _():
        tail_copy().wait_send()

    @pl.when(near)
    def _():
        @pl.loop(0, groups)
        def _(g):
            for copy in near_copies(g):
                copy.wait_send()

    @pl.when(far)
    def _():
        @pl.loop(0, groups)
        def _(g):
            for copy in far_copies(g):
                copy.wait_send()

    @pl.when(relays)
    def _():
        @pl.loop(0, groups)
        def _(g):
            for copy in relay_copies(g):
                copy.wait_send()

    @pl.loop(0, n)
    def _(i):
        dp_copy(i).wait_send()

    @pl.loop(0, n - 1)
    def _(i):
        rs_copy(i, owner_at(i)).wait_send()

    @pl.loop(1, n)
    def _(j):
        ag_copy(me, lax.rem(me + j, n)).wait_send()


def fused(inputs, feat_weight, filter_taps, upstream):
    x, up = inputs[0], upstream[0]
    n = lax.axis_size("ctx")
    rows, channels = up.shape
    filt_rows, reach = filter_taps.shape[0], feat_weight.shape[0]
    scale = (lax.axis_size("dp") * n * rows) ** (-0.5)
    mats = [jnp.asarray(m) for m in transforms(rows, filt_rows)]
    size = rows + filt_rows
    width = 2 * LANES
    packed = -(-(filt_rows + 3 * PAD) // 16) * 16
    dma = lambda *shape: pltpu.SemaphoreType.DMA(shape)
    return pl.pallas_call(
        functools.partial(fused_kernel, reach, scale),
        out_shape=[
            jax.ShapeDtypeStruct(filter_taps.shape, F32),
            jax.ShapeDtypeStruct(feat_weight.shape, F32),
        ],
        in_specs=[pl.BlockSpec(memory_space=pltpu.VMEM)] * 8,
        out_specs=[pl.BlockSpec(memory_space=pltpu.VMEM)] * 2,
        scratch_shapes=[
            pltpu.VMEM((filt_rows, channels), F32),
            pltpu.VMEM((reach, x.shape[1]), F32),
            pltpu.VMEM((PAD, x.shape[1]), BF16),
            pltpu.VMEM((PAD, x.shape[1]), BF16),
            pltpu.VMEM((filt_rows, channels), BF16),
            pltpu.VMEM((filt_rows, channels), BF16),
            pltpu.VMEM((filt_rows, channels), BF16),
            pltpu.VMEM((filt_rows, channels), BF16),
            pltpu.VMEM((PAD + size, width), F32),
            pltpu.VMEM((PAD + rows, width), F32),
            pltpu.VMEM((PAD + rows, width), F32),
            pltpu.VMEM((size, width), BF16),
            pltpu.VMEM((n, 2, packed, LANES), F32),
            pltpu.VMEM((n, packed, LANES), F32),
            pltpu.VMEM((n, packed, LANES), BF16),
            pltpu.VMEM((n, packed, LANES), BF16),
            pltpu.VMEM((n, packed, LANES), BF16),
            dma(2), dma(2), dma(2),
            pltpu.SemaphoreType.DMA, pltpu.SemaphoreType.DMA,
            *[dma(n // GROUP, 4)] * 4,
            dma(n), dma(n), dma(n), dma(n), dma(n), dma(n),
        ],
        compiler_params=pltpu.CompilerParams(
            collective_id=0, has_side_effects=True, vmem_limit_bytes=60 * 2**20
        ),
    )(x, up, filter_taps, feat_weight, *mats)


def per_device(inputs, feat_weight, filter_taps, upstream):
    n = lax.axis_size("ctx")
    cut = 2 * n * LANES
    whole = n % GROUP == 0 and n % PLANE == 0 and PLANE % GROUP == 0
    if lax.axis_size("dp") == 2 and upstream.shape[2] == cut and whole:
        return fused(inputs, feat_weight, filter_taps, upstream)
    return by_collectives(inputs, feat_weight, filter_taps, upstream)


def solution(mesh):
    placed = (P("dp", "ctx", None), P(None, "dp"), P(None, "dp"), P("dp", "ctx", None))
    return jax.shard_map(
        per_device,
        mesh=mesh,
        in_specs=placed,
        out_specs=(P(None, "dp"), P(None, "dp")),
        check_vma=False,
    )
```

```python
import functools

import jax
import jax.numpy as jnp
import numpy as np
from jax import lax
from jax.experimental import pallas as pl
from jax.experimental.pallas import tpu as pltpu
from jax.sharding import PartitionSpec as P

PAD = 8
F32 = jnp.float32
BF16 = jnp.bfloat16


def from_behind(block, axis, distance):
    devices = range(lax.axis_size(axis))
    route = [(i - distance, i) for i in devices if i - distance in devices]
    return lax.ppermute(block, axis, route)


def two_parts(matrix):
    high = matrix.astype(BF16)
    low = (matrix - high.astype(np.float64)).astype(BF16)
    return high, low


def transforms(rows, taps):
    size = rows + taps
    half = size // 2
    angle = 2 * np.pi * np.outer(np.arange(half), np.arange(size)) / size
    cosines = np.cos(angle)
    sines = -np.sin(angle)
    sines[0] = np.cos(np.pi * np.arange(size))
    forward = np.concatenate([cosines, sines], 0)
    weight = np.full((size, 1), 2.0 / size)
    weight[0] = weight[half] = 1.0 / size
    backward = (forward * weight).T
    f_high, f_low = two_parts(forward)
    b_high, b_low = two_parts(backward)
    cat = lambda *parts: np.concatenate(parts, 1)
    return (
        cat(f_high[:, :rows], f_low[:, :rows]),
        cat(f_high[:, :taps], f_low[:, :taps], f_high[:, :taps]),
        cat(f_high, f_low),
        cat(b_high, b_low),
    )


def dot(a, b):
    return jnp.dot(a, b, preferred_element_type=F32)


def chunk_terms(q_ext, k_ext, v_ext, up_ext, taps, weights, mats, rows, reach):
    to_mixed, to_taps, to_grad, back = mats
    size = up_ext.shape[0]
    half = size // 2

    def featured(ext, w, out_rows):
        total = w[0:1] * ext[PAD : PAD + out_rows, :]
        for j in range(1, reach):
            total += w[j : j + 1] * ext[PAD - j : PAD - j + out_rows, :]
        return total

    def lagged(grad, ext, out_rows):
        sums = [
            jnp.sum(grad * ext[PAD - j : PAD - j + out_rows, :], 0, keepdims=True)
            for j in range(reach)
        ]
        sums += [jnp.zeros_like(sums[0])] * (PAD - reach)
        return jnp.concatenate(sums, 0)

    key_part = featured(k_ext, weights[1], rows)
    value_part = featured(v_ext, weights[2], rows)
    mixed = (key_part * value_part).astype(BF16)
    m_hat = dot(to_mixed[...], jnp.concatenate([mixed, mixed], 0))
    taps_high = taps.astype(BF16)
    taps_low = (taps - taps_high.astype(F32)).astype(BF16)
    t_hat = dot(to_taps[...], jnp.concatenate([taps_high, taps_high, taps_low], 0))
    query = featured(q_ext, weights[0], size)
    grad_conv = (up_ext[...].astype(F32) * query).astype(BF16)
    g_hat = dot(to_grad[...], jnp.concatenate([grad_conv, grad_conv], 0))

    m_re, m_im = m_hat[:half], m_hat[half:]
    t_re, t_im = t_hat[:half], t_hat[half:]
    g_re, g_im = g_hat[:half], g_hat[half:]
    first = lax.broadcasted_iota(jnp.int32, m_re.shape, 0) == 0
    t_imz = jnp.where(first, 0.0, t_im)
    t_ren = jnp.where(first, t_im, t_re)
    m_imz = jnp.where(first, 0.0, m_im)
    m_ren = jnp.where(first, m_im, m_re)

    def inverse(re, im, out_rows):
        re, im = re.astype(BF16), im.astype(BF16)
        return dot(back[:out_rows, :], jnp.concatenate([re, im, re, im], 0))

    conv_out = inverse(
        m_re * t_re - m_im * t_imz, m_re * t_imz + m_im * t_ren, size
    )
    grad_mixed = inverse(
        g_re * t_re + g_im * t_imz, g_im * t_ren - g_re * t_imz, rows
    )
    filter_part = inverse(
        g_re * m_re + g_im * m_imz, g_im * m_ren - g_re * m_imz, taps.shape[0]
    )
    return (
        filter_part,
        lagged(up_ext[...].astype(F32) * conv_out, q_ext, size),
        lagged(grad_mixed * value_part, k_ext, rows),
        lagged(grad_mixed * key_part, v_ext, rows),
    )


def local_kernel(
    reach, xq, xk, xv, pq, pk, pv, nq, up, nup, taps, wq, wk, wv, m0, m1, m2, m3,
    filt, fq, fk, fv, q_ext, k_ext, v_ext, up_ext,
):
    rows = xq.shape[0]
    size = up_ext.shape[0]
    for ext, prev, block in ((q_ext, pq, xq), (k_ext, pk, xk), (v_ext, pv, xv)):
        ext[0:PAD, :] = prev[...].astype(F32)
        ext[PAD : PAD + rows, :] = block[...].astype(F32)
    q_ext[PAD + rows : PAD + size, :] = nq[...].astype(F32)
    up_ext[0:rows, :] = up[...]
    up_ext[rows:size, :] = nup[...]
    filt[...], fq[...], fk[...], fv[...] = chunk_terms(
        q_ext, k_ext, v_ext, up_ext, taps[...], (wq[...], wk[...], wv[...]),
        (m0, m1, m2, m3), rows, reach,
    )


def by_collectives(inputs, feat_weight, filter_taps, upstream):
    inputs_here = inputs[0]
    grad_here = upstream[0]
    rows = inputs_here.shape[0]
    channels = grad_here.shape[1]
    filt_rows = filter_taps.shape[0]
    reach = feat_weight.shape[0]
    scale = (lax.axis_size("dp") * lax.axis_size("ctx") * rows) ** (-0.5)
    feat_full, taps_full = (
        lax.all_gather(feat_weight, "dp", axis=1, tiled=True),
        lax.all_gather(filter_taps, "dp", axis=1, tiled=True),
    )
    next_grad, next_query = from_behind(
        (grad_here[:filt_rows], inputs_here[:filt_rows, :channels]), "ctx", -1
    )
    before = from_behind(inputs_here[rows - PAD :], "ctx", 1)
    weights = jnp.concatenate(
        [feat_full, jnp.zeros((PAD - reach, feat_full.shape[1]), F32)], 0
    )
    mats = [jnp.asarray(m) for m in transforms(rows, filt_rows)]
    width = 256
    steps = channels // width
    size = rows + filt_rows
    part = lambda r, group: pl.BlockSpec((r, width), lambda i: (0, i + group * steps))
    whole = lambda m: pl.BlockSpec(m.shape, lambda i: (0, 0))
    out = lambda r: jax.ShapeDtypeStruct((r, channels), F32)
    filter_part, feat_q, feat_k, feat_v = pl.pallas_call(
        functools.partial(local_kernel, reach),
        grid=(steps,),
        out_shape=[out(filt_rows), out(PAD), out(PAD), out(PAD)],
        in_specs=[part(rows, g) for g in range(3)]
        + [part(PAD, g) for g in range(3)]
        + [part(filt_rows, 0), part(rows, 0), part(filt_rows, 0), part(filt_rows, 0)]
        + [part(PAD, g) for g in range(3)]
        + [whole(m) for m in mats],
        out_specs=[part(filt_rows, 0)] + [part(PAD, 0)] * 3,
        scratch_shapes=[
            pltpu.VMEM((PAD + size, width), F32),
            pltpu.VMEM((PAD + rows, width), F32),
            pltpu.VMEM((PAD + rows, width), F32),
            pltpu.VMEM((size, width), BF16),
        ],
    )(
        inputs_here, inputs_here, inputs_here, before, before, before, next_query,
        grad_here, next_grad, taps_full, weights, weights, weights, *mats,
    )
    feat_part = jnp.concatenate([feat_q, feat_k, feat_v], 1)[:reach]
    filter_summed, feat_summed = (
        lax.psum_scatter(filter_part, "dp", scatter_dimension=1, tiled=True),
        lax.psum_scatter(feat_part, "dp", scatter_dimension=1, tiled=True),
    )
    filter_whole, feat_whole = lax.psum((filter_summed, feat_summed), "ctx")
    return (filter_whole * scale, feat_whole * scale)


MESH = pl.DeviceIdType.MESH
LANES = 128
GROUP = 2
PLANE = 4


def fused_kernel(
    reach, scale, x, up, taps_here, w_here, m0, m1, m2, m3, filt_out, feat_out,
    taps_all, w_all, tail, prev, n_up, n_q, r_up, r_q, q_ext, k_ext, v_ext, up_ext,
    stage, dp_got, rs_send, rs_got, gathered,
    own_sem, swap_send, swap_got, tail_send, tail_got, halo_send, halo_got,
    relay_send, relay_got,
    dp_send, dp_recv, rs_ssem, rs_rsem, ag_ssem, ag_rsem,
):
    n = lax.axis_size("ctx")
    me, core = lax.axis_index("ctx"), lax.axis_index("dp")
    rows, filt_rows = x.shape[0], taps_here.shape[0]
    channels = up.shape[1]
    half = channels // 2
    feat_half = w_here.shape[1]
    size = rows + filt_rows
    packed = stage.shape[2]
    partner = {"dp": 1 - core}

    barrier = pltpu.get_barrier_semaphore()
    pl.semaphore_signal(barrier, inc=1, device_id=partner, device_id_type=MESH)

    @pl.loop(1, n)
    def _(j):
        pl.semaphore_signal(
            barrier, inc=1, device_id={"ctx": lax.rem(me + j, n)}, device_id_type=MESH
        )

    def remote(src, dst, send, got, device):
        return pltpu.make_async_remote_copy(
            src_ref=src, dst_ref=dst, send_sem=send, recv_sem=got,
            device_id=device, device_id_type=MESH,
        )

    def lanes_of(owner, piece):
        return pl.ds(pl.multiple_of(owner * LANES + piece * half, LANES), LANES)

    def swaps():
        taps_side = pl.ds(pl.multiple_of(core * half, LANES), half)
        feat_side = pl.ds(pl.multiple_of(core * feat_half, LANES), feat_half)
        return (
            remote(taps_here, taps_all.at[:, taps_side], swap_send.at[0], swap_got.at[0], partner),
            remote(w_here, w_all.at[:, feat_side], swap_send.at[1], swap_got.at[1], partner),
        ), (
            pltpu.make_async_copy(taps_here, taps_all.at[:, taps_side], own_sem.at[0]),
            pltpu.make_async_copy(w_here, w_all.at[:, feat_side], own_sem.at[1]),
        )

    def tail_copy():
        return remote(tail, prev, tail_send, tail_got, {"ctx": lax.rem(me + 1, n)})

    groups = n // GROUP

    def block_copies(g, first, sources, targets, send, got, device):
        copies = []
        for piece in range(2):
            low = first * (GROUP * LANES) + piece * half
            at = pl.ds(pl.multiple_of(low, LANES), GROUP * LANES)
            for k, (src, dst) in enumerate(zip(sources, targets)):
                s = 2 * piece + k
                copies.append(
                    remote(
                        src.at[pl.ds(0, filt_rows), at], dst.at[:, at],
                        send.at[g, s], got.at[g, s], {"ctx": device},
                    )
                )
        return copies

    head, landing, relay = (up, x), (n_up, n_q), (r_up, r_q)
    near = (me > 0) & (lax.rem(me, PLANE) != 0)
    far = (me > 0) & (lax.rem(me, PLANE) == 0)
    relays = (lax.rem(me, PLANE) == 0) & (me < n - PLANE)

    def near_copies(g):
        back = lax.rem(me + n - 1, n)
        return block_copies(
            g, group_at(g, back), head, landing, halo_send, halo_got, back
        )

    def far_copies(g):
        back = lax.rem(me + n - 1, n)
        via = lax.rem(me + n - PLANE, n)
        return block_copies(g, group_at(g, back), head, relay, halo_send, relay_got, via)

    def arrivals(g):
        return block_copies(
            g, group_at(g, me), head, landing, halo_send, halo_got, lax.rem(me + 1, n)
        )

    def relay_arrivals(g):
        end = lax.rem(me + PLANE - 1, n)
        return block_copies(
            g, group_at(g, end), head, relay, halo_send, relay_got, lax.rem(me + PLANE, n)
        )

    def relay_copies(g):
        end = lax.rem(me + PLANE - 1, n)
        return block_copies(
            g, group_at(g, end), relay, landing, relay_send, halo_got, end
        )

    def group_at(g, device):
        return lax.rem(g + 1 + device // GROUP, groups)

    sent, kept = swaps()
    for copy in kept:
        copy.start()

    tail[...] = x[rows - PAD :, :]

    @pl.when(me == 0)
    def _():
        prev[...] = jnp.zeros_like(prev)

    @pl.when(me == n - 1)
    def _():
        n_up[...] = jnp.zeros_like(n_up)
        n_q[...] = jnp.zeros_like(n_q)

    pl.semaphore_wait(barrier, n)
    for copy in sent:
        copy.start()

    @pl.when(me < n - 1)
    def _():
        tail_copy().start()

    @pl.when(near)
    def _():
        @pl.loop(0, groups)
        def _(g):
            for copy in near_copies(g):
                copy.start()

    @pl.when(far)
    def _():
        @pl.loop(0, groups)
        def _(g):
            for copy in far_copies(g):
                copy.start()

    for copy in kept:
        copy.wait()
    for copy in sent:
        copy.wait()

    @pl.when(me > 0)
    def _():
        tail_copy().wait_recv()

    def dp_copy(i):
        return remote(
            stage.at[i, 1 - core], dp_got.at[i], dp_send.at[i], dp_recv.at[i], partner
        )

    def rs_copy(i, owner):
        return remote(
            rs_send.at[i], rs_got.at[me], rs_ssem.at[i], rs_rsem.at[me], {"ctx": owner}
        )

    def owner_at(i):
        return group_at(i // GROUP, me) * GROUP + lax.rem(i + 1 + me, GROUP)

    def compute(i):
        owner = owner_at(i)

        @pl.when(relays & (lax.rem(i, GROUP) == 0))
        def _():
            g = i // GROUP
            for came, goes in zip(relay_arrivals(g), relay_copies(g)):
                came.wait_recv()
                goes.start()

        @pl.when((me < n - 1) & (lax.rem(i, GROUP) == 0))
        def _():
            for copy in arrivals(i // GROUP):
                copy.wait_recv()

        def both(ref, group):
            return jnp.concatenate(
                [ref[:, pl.ds(pl.multiple_of(group * channels + p * half + owner * LANES, LANES), LANES)] for p in range(2)],
                1,
            )

        for group, ext in enumerate((q_ext, k_ext, v_ext)):
            ext[0:PAD, :] = both(prev, group).astype(F32)
            ext[PAD : PAD + rows, :] = both(x, group).astype(F32)
        q_ext[PAD + rows : PAD + size, :] = both(n_q, 0).astype(F32)
        up_ext[0:rows, :] = both(up, 0)
        up_ext[rows:size, :] = both(n_up, 0)
        filt, feat_q, feat_k, feat_v = chunk_terms(
            q_ext, k_ext, v_ext, up_ext, both(taps_all, 0),
            [both(w_all, group) for group in range(3)],
            (m0, m1, m2, m3), rows, reach,
        )
        a, b = slice(0, LANES), slice(LANES, 2 * LANES)
        rest = [jnp.zeros((packed - filt_rows - 3 * PAD, LANES), F32)]
        stage[i, 0] = jnp.concatenate(
            [filt[:, a], feat_q[:, a], feat_q[:, b], feat_k[:, a]] + rest, 0
        )
        stage[i, 1] = jnp.concatenate(
            [filt[:, b], feat_k[:, b], feat_v[:, a], feat_v[:, b]] + rest, 0
        )
        dp_copy(i).start()

    def reduce_pair(i):
        dp_copy(i).wait_recv()
        return (stage[i, core] + dp_got[i]).astype(BF16)

    def send_on(i):
        rs_send[i] = reduce_pair(i)
        rs_copy(i, owner_at(i)).start()

    @pl.loop(0, n)
    def _(i):
        compute(i)

        @pl.when(i > 0)
        def _():
            send_on(i - 1)

    total = reduce_pair(n - 1).astype(F32)
    for j in range(1, n):
        src = lax.rem(me + j, n)
        remote(
            rs_send.at[0], rs_got.at[src], rs_ssem.at[0], rs_rsem.at[src], {"ctx": src}
        ).wait_recv()
        total += rs_got[src].astype(F32)
    gathered[me] = total.astype(BF16)

    planes = n // PLANE

    def ag_copy(k, q):
        owner = lax.rem(me + k * PLANE, n)
        target = me // PLANE * PLANE + lax.rem(me + q, PLANE)
        return remote(
            gathered.at[owner], gathered.at[owner], ag_ssem.at[k, q], ag_rsem.at[owner],
            {"ctx": target},
        )

    def ag_column(k):
        return remote(
            gathered.at[me], gathered.at[me], ag_ssem.at[k, 0], ag_rsem.at[me],
            {"ctx": lax.rem(me + k * PLANE, n)},
        )

    def ag_arrival(owner):
        return remote(
            gathered.at[owner], gathered.at[owner], ag_ssem.at[0, 0], ag_rsem.at[owner],
            {"ctx": lax.rem(me + 1, n)},
        )

    @pl.loop(1, planes)
    def _(k):
        ag_column(k).start()

    @pl.loop(1, PLANE)
    def _(q):
        ag_copy(0, q).start()

    def unpack(owner):
        value = gathered[owner].astype(F32) * scale
        filt_out[:, pl.ds(pl.multiple_of(owner * LANES, LANES), LANES)] = value[:filt_rows]
        for g in range(3):
            low = filt_rows + g * PAD
            at = pl.ds(pl.multiple_of(owner * LANES + g * half, LANES), LANES)
            feat_out[:, at] = value[low : low + reach]

    unpack(me)

    @pl.loop(1, planes)
    def _(k):
        src = lax.rem(me + k * PLANE, n)
        ag_arrival(src).wait_recv()

        @pl.loop(1, PLANE)
        def _(q):
            ag_copy(k, q).start()

        unpack(src)

    @pl.loop(0, planes)
    def _(k):
        @pl.loop(1, PLANE)
        def _(q):
            low = lax.rem(me // PLANE + k, planes) * PLANE
            src = low + lax.rem(me + q, PLANE)
            ag_arrival(src).wait_recv()
            unpack(src)

    @pl.when(me < n - 1)
    def _():
        tail_copy().wait_send()

    @pl.when(near)
    def _():
        @pl.loop(0, groups)
        def _(g):
            for copy in near_copies(g):
                copy.wait_send()

    @pl.when(far)
    def _():
        @pl.loop(0, groups)
        def _(g):
            for copy in far_copies(g):
                copy.wait_send()

    @pl.when(relays)
    def _():
        @pl.loop(0, groups)
        def _(g):
            for copy in relay_copies(g):
                copy.wait_send()

    @pl.loop(0, n)
    def _(i):
        dp_copy(i).wait_send()

    @pl.loop(0, n - 1)
    def _(i):
        rs_copy(i, owner_at(i)).wait_send()

    @pl.loop(1, planes)
    def _(k):
        ag_column(k).wait_send()

    @pl.loop(0, planes)
    def _(k):
        @pl.loop(1, PLANE)
        def _(q):
            ag_copy(k, q).wait_send()


def fused(inputs, feat_weight, filter_taps, upstream):
    x, up = inputs[0], upstream[0]
    n = lax.axis_size("ctx")
    rows, channels = up.shape
    filt_rows, reach = filter_taps.shape[0], feat_weight.shape[0]
    scale = (lax.axis_size("dp") * n * rows) ** (-0.5)
    mats = [jnp.asarray(m) for m in transforms(rows, filt_rows)]
    size = rows + filt_rows
    width = 2 * LANES
    packed = -(-(filt_rows + 3 * PAD) // 16) * 16
    dma = lambda *shape: pltpu.SemaphoreType.DMA(shape)
    return pl.pallas_call(
        functools.partial(fused_kernel, reach, scale),
        out_shape=[
            jax.ShapeDtypeStruct(filter_taps.shape, F32),
            jax.ShapeDtypeStruct(feat_weight.shape, F32),
        ],
        in_specs=[pl.BlockSpec(memory_space=pltpu.VMEM)] * 8,
        out_specs=[pl.BlockSpec(memory_space=pltpu.VMEM)] * 2,
        scratch_shapes=[
            pltpu.VMEM((filt_rows, channels), F32),
            pltpu.VMEM((reach, x.shape[1]), F32),
            pltpu.VMEM((PAD, x.shape[1]), BF16),
            pltpu.VMEM((PAD, x.shape[1]), BF16),
            pltpu.VMEM((filt_rows, channels), BF16),
            pltpu.VMEM((filt_rows, channels), BF16),
            pltpu.VMEM((filt_rows, channels), BF16),
            pltpu.VMEM((filt_rows, channels), BF16),
            pltpu.VMEM((PAD + size, width), F32),
            pltpu.VMEM((PAD + rows, width), F32),
            pltpu.VMEM((PAD + rows, width), F32),
            pltpu.VMEM((size, width), BF16),
            pltpu.VMEM((n, 2, packed, LANES), F32),
            pltpu.VMEM((n, packed, LANES), F32),
            pltpu.VMEM((n, packed, LANES), BF16),
            pltpu.VMEM((n, packed, LANES), BF16),
            pltpu.VMEM((n, packed, LANES), BF16),
            dma(2), dma(2), dma(2),
            pltpu.SemaphoreType.DMA, pltpu.SemaphoreType.DMA,
            *[dma(n // GROUP, 4)] * 4,
            dma(n), dma(n), dma(n), dma(n), dma(n // PLANE, PLANE), dma(n),
        ],
        compiler_params=pltpu.CompilerParams(
            collective_id=0, has_side_effects=True, vmem_limit_bytes=60 * 2**20
        ),
    )(x, up, filter_taps, feat_weight, *mats)


def per_device(inputs, feat_weight, filter_taps, upstream):
    n = lax.axis_size("ctx")
    cut = 2 * n * LANES
    whole = n % GROUP == 0 and n % PLANE == 0 and PLANE % GROUP == 0
    if lax.axis_size("dp") == 2 and upstream.shape[2] == cut and whole:
        return fused(inputs, feat_weight, filter_taps, upstream)
    return by_collectives(inputs, feat_weight, filter_taps, upstream)


def solution(mesh):
    placed = (P("dp", "ctx", None), P(None, "dp"), P(None, "dp"), P("dp", "ctx", None))
    return jax.shard_map(
        per_device,
        mesh=mesh,
        in_specs=placed,
        out_specs=(P(None, "dp"), P(None, "dp")),
        check_vma=False,
    )
```

```python
import functools

import jax
import jax.numpy as jnp
import numpy as np
from jax import lax
from jax.experimental import pallas as pl
from jax.experimental.pallas import tpu as pltpu
from jax.sharding import PartitionSpec as P

PAD = 8
F32 = jnp.float32
BF16 = jnp.bfloat16


def from_behind(block, axis, distance):
    devices = range(lax.axis_size(axis))
    route = [(i - distance, i) for i in devices if i - distance in devices]
    return lax.ppermute(block, axis, route)


def two_parts(matrix):
    high = matrix.astype(BF16)
    low = (matrix - high.astype(np.float64)).astype(BF16)
    return high, low


def transforms(rows, taps):
    size = rows + taps
    half = size // 2
    angle = 2 * np.pi * np.outer(np.arange(half), np.arange(size)) / size
    cosines = np.cos(angle)
    sines = -np.sin(angle)
    sines[0] = np.cos(np.pi * np.arange(size))
    forward = np.concatenate([cosines, sines], 0)
    weight = np.full((size, 1), 2.0 / size)
    weight[0] = weight[half] = 1.0 / size
    backward = (forward * weight).T
    f_high, f_low = two_parts(forward)
    b_high, b_low = two_parts(backward)
    cat = lambda *parts: np.concatenate(parts, 1)
    return (
        cat(f_high[:, :rows], f_low[:, :rows]),
        cat(f_high[:, :taps], f_low[:, :taps], f_high[:, :taps]),
        cat(f_high, f_low),
        cat(b_high, b_low),
    )


def dot(a, b):
    return jnp.dot(a, b, preferred_element_type=F32)


def chunk_terms(q_ext, k_ext, v_ext, up_ext, taps, weights, mats, rows, reach):
    to_mixed, to_taps, to_grad, back = mats
    size = up_ext.shape[0]
    half = size // 2

    def featured(ext, w, out_rows):
        total = w[0:1] * ext[PAD : PAD + out_rows, :]
        for j in range(1, reach):
            total += w[j : j + 1] * ext[PAD - j : PAD - j + out_rows, :]
        return total

    def lagged(grad, ext, out_rows):
        sums = [
            jnp.sum(grad * ext[PAD - j : PAD - j + out_rows, :], 0, keepdims=True)
            for j in range(reach)
        ]
        sums += [jnp.zeros_like(sums[0])] * (PAD - reach)
        return jnp.concatenate(sums, 0)

    key_part = featured(k_ext, weights[1], rows)
    value_part = featured(v_ext, weights[2], rows)
    mixed = (key_part * value_part).astype(BF16)
    m_hat = dot(to_mixed[...], jnp.concatenate([mixed, mixed], 0))
    taps_high = taps.astype(BF16)
    taps_low = (taps - taps_high.astype(F32)).astype(BF16)
    t_hat = dot(to_taps[...], jnp.concatenate([taps_high, taps_high, taps_low], 0))
    query = featured(q_ext, weights[0], size)
    grad_conv = (up_ext[...].astype(F32) * query).astype(BF16)
    g_hat = dot(to_grad[...], jnp.concatenate([grad_conv, grad_conv], 0))

    m_re, m_im = m_hat[:half], m_hat[half:]
    t_re, t_im = t_hat[:half], t_hat[half:]
    g_re, g_im = g_hat[:half], g_hat[half:]
    first = lax.broadcasted_iota(jnp.int32, m_re.shape, 0) == 0
    t_imz = jnp.where(first, 0.0, t_im)
    t_ren = jnp.where(first, t_im, t_re)
    m_imz = jnp.where(first, 0.0, m_im)
    m_ren = jnp.where(first, m_im, m_re)

    def inverse(re, im, out_rows):
        re, im = re.astype(BF16), im.astype(BF16)
        return dot(back[:out_rows, :], jnp.concatenate([re, im, re, im], 0))

    conv_out = inverse(
        m_re * t_re - m_im * t_imz, m_re * t_imz + m_im * t_ren, size
    )
    grad_mixed = inverse(
        g_re * t_re + g_im * t_imz, g_im * t_ren - g_re * t_imz, rows
    )
    filter_part = inverse(
        g_re * m_re + g_im * m_imz, g_im * m_ren - g_re * m_imz, taps.shape[0]
    )
    return (
        filter_part,
        lagged(up_ext[...].astype(F32) * conv_out, q_ext, size),
        lagged(grad_mixed * value_part, k_ext, rows),
        lagged(grad_mixed * key_part, v_ext, rows),
    )


def local_kernel(
    reach, xq, xk, xv, pq, pk, pv, nq, up, nup, taps, wq, wk, wv, m0, m1, m2, m3,
    filt, fq, fk, fv, q_ext, k_ext, v_ext, up_ext,
):
    rows = xq.shape[0]
    size = up_ext.shape[0]
    for ext, prev, block in ((q_ext, pq, xq), (k_ext, pk, xk), (v_ext, pv, xv)):
        ext[0:PAD, :] = prev[...].astype(F32)
        ext[PAD : PAD + rows, :] = block[...].astype(F32)
    q_ext[PAD + rows : PAD + size, :] = nq[...].astype(F32)
    up_ext[0:rows, :] = up[...]
    up_ext[rows:size, :] = nup[...]
    filt[...], fq[...], fk[...], fv[...] = chunk_terms(
        q_ext, k_ext, v_ext, up_ext, taps[...], (wq[...], wk[...], wv[...]),
        (m0, m1, m2, m3), rows, reach,
    )


def by_collectives(inputs, feat_weight, filter_taps, upstream):
    inputs_here = inputs[0]
    grad_here = upstream[0]
    rows = inputs_here.shape[0]
    channels = grad_here.shape[1]
    filt_rows = filter_taps.shape[0]
    reach = feat_weight.shape[0]
    scale = (lax.axis_size("dp") * lax.axis_size("ctx") * rows) ** (-0.5)
    feat_full, taps_full = (
        lax.all_gather(feat_weight, "dp", axis=1, tiled=True),
        lax.all_gather(filter_taps, "dp", axis=1, tiled=True),
    )
    next_grad, next_query = from_behind(
        (grad_here[:filt_rows], inputs_here[:filt_rows, :channels]), "ctx", -1
    )
    before = from_behind(inputs_here[rows - PAD :], "ctx", 1)
    weights = jnp.concatenate(
        [feat_full, jnp.zeros((PAD - reach, feat_full.shape[1]), F32)], 0
    )
    mats = [jnp.asarray(m) for m in transforms(rows, filt_rows)]
    width = 256
    steps = channels // width
    size = rows + filt_rows
    part = lambda r, group: pl.BlockSpec((r, width), lambda i: (0, i + group * steps))
    whole = lambda m: pl.BlockSpec(m.shape, lambda i: (0, 0))
    out = lambda r: jax.ShapeDtypeStruct((r, channels), F32)
    filter_part, feat_q, feat_k, feat_v = pl.pallas_call(
        functools.partial(local_kernel, reach),
        grid=(steps,),
        out_shape=[out(filt_rows), out(PAD), out(PAD), out(PAD)],
        in_specs=[part(rows, g) for g in range(3)]
        + [part(PAD, g) for g in range(3)]
        + [part(filt_rows, 0), part(rows, 0), part(filt_rows, 0), part(filt_rows, 0)]
        + [part(PAD, g) for g in range(3)]
        + [whole(m) for m in mats],
        out_specs=[part(filt_rows, 0)] + [part(PAD, 0)] * 3,
        scratch_shapes=[
            pltpu.VMEM((PAD + size, width), F32),
            pltpu.VMEM((PAD + rows, width), F32),
            pltpu.VMEM((PAD + rows, width), F32),
            pltpu.VMEM((size, width), BF16),
        ],
    )(
        inputs_here, inputs_here, inputs_here, before, before, before, next_query,
        grad_here, next_grad, taps_full, weights, weights, weights, *mats,
    )
    feat_part = jnp.concatenate([feat_q, feat_k, feat_v], 1)[:reach]
    filter_summed, feat_summed = (
        lax.psum_scatter(filter_part, "dp", scatter_dimension=1, tiled=True),
        lax.psum_scatter(feat_part, "dp", scatter_dimension=1, tiled=True),
    )
    filter_whole, feat_whole = lax.psum((filter_summed, feat_summed), "ctx")
    return (filter_whole * scale, feat_whole * scale)


MESH = pl.DeviceIdType.MESH
LANES = 128
GROUP = 2
PLANE = 4
AHEAD = 4


def fused_kernel(
    reach, scale, x, up, taps_here, w_here, m0, m1, m2, m3, filt_out, feat_out,
    taps_all, w_all, tail, prev, n_up, n_q, r_up, r_q, q_ext, k_ext, v_ext, up_ext,
    stage, dp_got, rs_send, rs_got, gathered,
    own_sem, swap_send, swap_got, tail_send, tail_got, halo_send, halo_got,
    relay_send, relay_got,
    dp_send, dp_recv, rs_ssem, rs_rsem, ag_ssem, ag_rsem,
):
    n = lax.axis_size("ctx")
    me, core = lax.axis_index("ctx"), lax.axis_index("dp")
    rows, filt_rows = x.shape[0], taps_here.shape[0]
    channels = up.shape[1]
    half = channels // 2
    feat_half = w_here.shape[1]
    size = rows + filt_rows
    packed = stage.shape[2]
    partner = {"dp": 1 - core}

    barrier = pltpu.get_barrier_semaphore()
    pl.semaphore_signal(barrier, inc=1, device_id=partner, device_id_type=MESH)

    @pl.loop(1, n)
    def _(j):
        pl.semaphore_signal(
            barrier, inc=1, device_id={"ctx": lax.rem(me + j, n)}, device_id_type=MESH
        )

    def remote(src, dst, send, got, device):
        return pltpu.make_async_remote_copy(
            src_ref=src, dst_ref=dst, send_sem=send, recv_sem=got,
            device_id=device, device_id_type=MESH,
        )

    def lanes_of(owner, piece):
        return pl.ds(pl.multiple_of(owner * LANES + piece * half, LANES), LANES)

    def swaps():
        taps_side = pl.ds(pl.multiple_of(core * half, LANES), half)
        feat_side = pl.ds(pl.multiple_of(core * feat_half, LANES), feat_half)
        return (
            remote(taps_here, taps_all.at[:, taps_side], swap_send.at[0], swap_got.at[0], partner),
            remote(w_here, w_all.at[:, feat_side], swap_send.at[1], swap_got.at[1], partner),
        ), (
            pltpu.make_async_copy(taps_here, taps_all.at[:, taps_side], own_sem.at[0]),
            pltpu.make_async_copy(w_here, w_all.at[:, feat_side], own_sem.at[1]),
        )

    def tail_copy():
        return remote(tail, prev, tail_send, tail_got, {"ctx": lax.rem(me + 1, n)})

    groups = n // GROUP

    def block_copies(g, first, sources, targets, send, got, device):
        copies = []
        for piece in range(2):
            low = first * (GROUP * LANES) + piece * half
            at = pl.ds(pl.multiple_of(low, LANES), GROUP * LANES)
            for k, (src, dst) in enumerate(zip(sources, targets)):
                s = 2 * piece + k
                copies.append(
                    remote(
                        src.at[pl.ds(0, filt_rows), at], dst.at[:, at],
                        send.at[g, s], got.at[g, s], {"ctx": device},
                    )
                )
        return copies

    head, landing, relay = (up, x), (n_up, n_q), (r_up, r_q)
    near = (me > 0) & (lax.rem(me, PLANE) != 0)
    far = (me > 0) & (lax.rem(me, PLANE) == 0)
    relays = (lax.rem(me, PLANE) == 0) & (me < n - PLANE)

    def near_copies(g):
        back = lax.rem(me + n - 1, n)
        return block_copies(
            g, group_at(g, back), head, landing, halo_send, halo_got, back
        )

    def far_copies(g):
        back = lax.rem(me + n - 1, n)
        via = lax.rem(me + n - PLANE, n)
        return block_copies(g, group_at(g, back), head, relay, halo_send, relay_got, via)

    def arrivals(g):
        return block_copies(
            g, group_at(g, me), head, landing, halo_send, halo_got, lax.rem(me + 1, n)
        )

    def relay_arrivals(g):
        end = lax.rem(me + PLANE - 1, n)
        return block_copies(
            g, group_at(g, end), head, relay, halo_send, relay_got, lax.rem(me + PLANE, n)
        )

    def relay_copies(g):
        end = lax.rem(me + PLANE - 1, n)
        return block_copies(
            g, group_at(g, end), relay, landing, relay_send, halo_got, end
        )

    def group_at(g, device):
        return lax.rem(g + 1 + device // GROUP, groups)

    sent, kept = swaps()
    for copy in kept:
        copy.start()

    tail[...] = x[rows - PAD :, :]

    @pl.when(me == 0)
    def _():
        prev[...] = jnp.zeros_like(prev)

    @pl.when(me == n - 1)
    def _():
        n_up[...] = jnp.zeros_like(n_up)
        n_q[...] = jnp.zeros_like(n_q)

    pl.semaphore_wait(barrier, n)
    for copy in sent:
        copy.start()

    @pl.when(me < n - 1)
    def _():
        tail_copy().start()

    @pl.when(near)
    def _():
        @pl.loop(0, min(AHEAD, groups))
        def _(g):
            for copy in near_copies(g):
                copy.start()

    @pl.when(far)
    def _():
        @pl.loop(0, min(AHEAD, groups))
        def _(g):
            for copy in far_copies(g):
                copy.start()

    for copy in kept:
        copy.wait()
    for copy in sent:
        copy.wait()

    @pl.when(me > 0)
    def _():
        tail_copy().wait_recv()

    def dp_copy(i):
        return remote(
            stage.at[i, 1 - core], dp_got.at[i], dp_send.at[i], dp_recv.at[i], partner
        )

    def rs_copy(i, owner):
        return remote(
            rs_send.at[i], rs_got.at[me], rs_ssem.at[i], rs_rsem.at[me], {"ctx": owner}
        )

    def owner_at(i):
        return group_at(i // GROUP, me) * GROUP + lax.rem(i + 1 + me, GROUP)

    def compute(i):
        owner = owner_at(i)

        @pl.when(relays & (lax.rem(i, GROUP) == 0))
        def _():
            g = i // GROUP
            for came, goes in zip(relay_arrivals(g), relay_copies(g)):
                came.wait_recv()
                goes.start()

        @pl.when(near & (lax.rem(i, GROUP) == 0) & (i // GROUP + AHEAD < groups))
        def _():
            for copy in near_copies(i // GROUP + AHEAD):
                copy.start()

        @pl.when(far & (lax.rem(i, GROUP) == 0) & (i // GROUP + AHEAD < groups))
        def _():
            for copy in far_copies(i // GROUP + AHEAD):
                copy.start()

        @pl.when((me < n - 1) & (lax.rem(i, GROUP) == 0))
        def _():
            for copy in arrivals(i // GROUP):
                copy.wait_recv()

        def both(ref, group):
            return jnp.concatenate(
                [ref[:, pl.ds(pl.multiple_of(group * channels + p * half + owner * LANES, LANES), LANES)] for p in range(2)],
                1,
            )

        for group, ext in enumerate((q_ext, k_ext, v_ext)):
            ext[0:PAD, :] = both(prev, group).astype(F32)
            ext[PAD : PAD + rows, :] = both(x, group).astype(F32)
        q_ext[PAD + rows : PAD + size, :] = both(n_q, 0).astype(F32)
        up_ext[0:rows, :] = both(up, 0)
        up_ext[rows:size, :] = both(n_up, 0)
        filt, feat_q, feat_k, feat_v = chunk_terms(
            q_ext, k_ext, v_ext, up_ext, both(taps_all, 0),
            [both(w_all, group) for group in range(3)],
            (m0, m1, m2, m3), rows, reach,
        )
        a, b = slice(0, LANES), slice(LANES, 2 * LANES)
        rest = [jnp.zeros((packed - filt_rows - 3 * PAD, LANES), F32)]
        stage[i, 0] = jnp.concatenate(
            [filt[:, a], feat_q[:, a], feat_q[:, b], feat_k[:, a]] + rest, 0
        )
        stage[i, 1] = jnp.concatenate(
            [filt[:, b], feat_k[:, b], feat_v[:, a], feat_v[:, b]] + rest, 0
        )
        dp_copy(i).start()

    def reduce_pair(i):
        dp_copy(i).wait_recv()
        return (stage[i, core] + dp_got[i]).astype(BF16)

    def send_on(i):
        rs_send[i] = reduce_pair(i)
        rs_copy(i, owner_at(i)).start()

    @pl.loop(0, n)
    def _(i):
        compute(i)

        @pl.when(i > 0)
        def _():
            send_on(i - 1)

    total = reduce_pair(n - 1).astype(F32)
    for j in range(1, n):
        src = lax.rem(me + j, n)
        remote(
            rs_send.at[0], rs_got.at[src], rs_ssem.at[0], rs_rsem.at[src], {"ctx": src}
        ).wait_recv()
        total += rs_got[src].astype(F32)
    gathered[me] = total.astype(BF16)

    planes = n // PLANE

    def ag_copy(k, q):
        owner = lax.rem(me + k * PLANE, n)
        target = me // PLANE * PLANE + lax.rem(me + q, PLANE)
        return remote(
            gathered.at[owner], gathered.at[owner], ag_ssem.at[k, q], ag_rsem.at[owner],
            {"ctx": target},
        )

    def ag_column(k):
        return remote(
            gathered.at[me], gathered.at[me], ag_ssem.at[k, 0], ag_rsem.at[me],
            {"ctx": lax.rem(me + k * PLANE, n)},
        )

    def ag_arrival(owner):
        return remote(
            gathered.at[owner], gathered.at[owner], ag_ssem.at[0, 0], ag_rsem.at[owner],
            {"ctx": lax.rem(me + 1, n)},
        )

    @pl.loop(1, planes)
    def _(k):
        ag_column(k).start()

    @pl.loop(1, PLANE)
    def _(q):
        ag_copy(0, q).start()

    def unpack(owner):
        value = gathered[owner].astype(F32) * scale
        filt_out[:, pl.ds(pl.multiple_of(owner * LANES, LANES), LANES)] = value[:filt_rows]
        for g in range(3):
            low = filt_rows + g * PAD
            at = pl.ds(pl.multiple_of(owner * LANES + g * half, LANES), LANES)
            feat_out[:, at] = value[low : low + reach]

    unpack(me)

    @pl.loop(1, planes)
    def _(k):
        src = lax.rem(me + k * PLANE, n)
        ag_arrival(src).wait_recv()

        @pl.loop(1, PLANE)
        def _(q):
            ag_copy(k, q).start()

        unpack(src)

    @pl.loop(0, planes)
    def _(k):
        @pl.loop(1, PLANE)
        def _(q):
            low = lax.rem(me // PLANE + k, planes) * PLANE
            src = low + lax.rem(me + q, PLANE)
            ag_arrival(src).wait_recv()
            unpack(src)

    @pl.when(me < n - 1)
    def _():
        tail_copy().wait_send()

    @pl.when(near)
    def _():
        @pl.loop(0, groups)
        def _(g):
            for copy in near_copies(g):
                copy.wait_send()

    @pl.when(far)
    def _():
        @pl.loop(0, groups)
        def _(g):
            for copy in far_copies(g):
                copy.wait_send()

    @pl.when(relays)
    def _():
        @pl.loop(0, groups)
        def _(g):
            for copy in relay_copies(g):
                copy.wait_send()

    @pl.loop(0, n)
    def _(i):
        dp_copy(i).wait_send()

    @pl.loop(0, n - 1)
    def _(i):
        rs_copy(i, owner_at(i)).wait_send()

    @pl.loop(1, planes)
    def _(k):
        ag_column(k).wait_send()

    @pl.loop(0, planes)
    def _(k):
        @pl.loop(1, PLANE)
        def _(q):
            ag_copy(k, q).wait_send()


def fused(inputs, feat_weight, filter_taps, upstream):
    x, up = inputs[0], upstream[0]
    n = lax.axis_size("ctx")
    rows, channels = up.shape
    filt_rows, reach = filter_taps.shape[0], feat_weight.shape[0]
    scale = (lax.axis_size("dp") * n * rows) ** (-0.5)
    mats = [jnp.asarray(m) for m in transforms(rows, filt_rows)]
    size = rows + filt_rows
    width = 2 * LANES
    packed = -(-(filt_rows + 3 * PAD) // 16) * 16
    dma = lambda *shape: pltpu.SemaphoreType.DMA(shape)
    return pl.pallas_call(
        functools.partial(fused_kernel, reach, scale),
        out_shape=[
            jax.ShapeDtypeStruct(filter_taps.shape, F32),
            jax.ShapeDtypeStruct(feat_weight.shape, F32),
        ],
        in_specs=[pl.BlockSpec(memory_space=pltpu.VMEM)] * 8,
        out_specs=[pl.BlockSpec(memory_space=pltpu.VMEM)] * 2,
        scratch_shapes=[
            pltpu.VMEM((filt_rows, channels), F32),
            pltpu.VMEM((reach, x.shape[1]), F32),
            pltpu.VMEM((PAD, x.shape[1]), BF16),
            pltpu.VMEM((PAD, x.shape[1]), BF16),
            pltpu.VMEM((filt_rows, channels), BF16),
            pltpu.VMEM((filt_rows, channels), BF16),
            pltpu.VMEM((filt_rows, channels), BF16),
            pltpu.VMEM((filt_rows, channels), BF16),
            pltpu.VMEM((PAD + size, width), F32),
            pltpu.VMEM((PAD + rows, width), F32),
            pltpu.VMEM((PAD + rows, width), F32),
            pltpu.VMEM((size, width), BF16),
            pltpu.VMEM((n, 2, packed, LANES), F32),
            pltpu.VMEM((n, packed, LANES), F32),
            pltpu.VMEM((n, packed, LANES), BF16),
            pltpu.VMEM((n, packed, LANES), BF16),
            pltpu.VMEM((n, packed, LANES), BF16),
            dma(2), dma(2), dma(2),
            pltpu.SemaphoreType.DMA, pltpu.SemaphoreType.DMA,
            *[dma(n // GROUP, 4)] * 4,
            dma(n), dma(n), dma(n), dma(n), dma(n // PLANE, PLANE), dma(n),
        ],
        compiler_params=pltpu.CompilerParams(
            collective_id=0, has_side_effects=True, vmem_limit_bytes=60 * 2**20
        ),
    )(x, up, filter_taps, feat_weight, *mats)


def per_device(inputs, feat_weight, filter_taps, upstream):
    n = lax.axis_size("ctx")
    cut = 2 * n * LANES
    whole = n % GROUP == 0 and n % PLANE == 0 and PLANE % GROUP == 0
    if lax.axis_size("dp") == 2 and upstream.shape[2] == cut and whole:
        return fused(inputs, feat_weight, filter_taps, upstream)
    return by_collectives(inputs, feat_weight, filter_taps, upstream)


def solution(mesh):
    placed = (P("dp", "ctx", None), P(None, "dp"), P(None, "dp"), P("dp", "ctx", None))
    return jax.shard_map(
        per_device,
        mesh=mesh,
        in_specs=placed,
        out_specs=(P(None, "dp"), P(None, "dp")),
        check_vma=False,
    )
```
